32 devices in a mesh: replica: 16 (over z, y, x), shard: 2 (over core).
Axes of the slice: x: 2, y: 2, z: 4, core: 2. Of those that a mesh axis runs over, the one named last changes fastest.
Arguments:
- block_input: float32 [10400, 1024], P(('replica', 'shard')), may hold values from -6 to 6
- norm1_gain: bfloat16 [1024], P('shard'), may hold values from 0.5 to 1.5
- norm1_bias: bfloat16 [1024], P('shard'), may hold values from -3 to 3
- qkv_weight: bfloat16 [1024, 3072], P('shard'), may hold values from -0.1875 to 0.1875
- query_bias: bfloat16 [1024], P('shard'), may hold values from -3 to 3
- value_bias: bfloat16 [1024], P('shard'), may hold values from -3 to 3
- proj_weight: bfloat16 [1024, 1024], P('shard'), may hold values from -0.75 to 0.75
- proj_bias: bfloat16 [1024], P('shard'), may hold values from -3 to 3
- attn_scale: bfloat16 [1024], P('shard'), may hold values from 0.29882812 to 1.5
- norm2_gain: bfloat16 [1024], P('shard'), may hold values from 0.5 to 1.5
- norm2_bias: bfloat16 [1024], P('shard'), may hold values from -3 to 3
- up_weight: bfloat16 [1024, 4096], P('shard'), may hold values from -0.1875 to 0.1875
- up_bias: bfloat16 [4096], P('shard'), may hold values from -3 to 3
- down_weight: bfloat16 [4096, 1024], P('shard'), may hold values from -0.09375 to 0.09375
- down_bias: bfloat16 [1024], P('shard'), may hold values from -3 to 3
- mlp_scale: bfloat16 [1024], P('shard'), may hold values from 0.29882812 to 1.5
- out_grad: float32 [10400, 1024], P(('replica', 'shard')), may hold values from -6 to 6
Outputs:
- block_output: float32 [10400, 1024], P(('replica', 'shard'))
- input_grad: float32 [10400, 1024], P(('replica', 'shard'))
- norm1_gain_grad: float32 [1024], P(('replica', 'shard'))
- norm1_bias_grad: float32 [1024], P(('replica', 'shard'))
- qkv_weight_grad: float32 [1024, 3072], P(('replica', 'shard'))
- query_bias_grad: float32 [1024], P(('replica', 'shard'))
- value_bias_grad: float32 [1024], P(('replica', 'shard'))
- proj_weight_grad: float32 [1024, 1024], P(('replica', 'shard'))
- proj_bias_grad: float32 [1024], P(('replica', 'shard'))
- attn_scale_grad: float32 [1024], P(('replica', 'shard'))
- norm2_gain_grad: float32 [1024], P(('replica', 'shard'))
- norm2_bias_grad: float32 [1024], P(('replica', 'shard'))
- up_weight_grad: float32 [1024, 4096], P(('replica', 'shard'))
- up_bias_grad: float32 [4096], P(('replica', 'shard'))
- down_weight_grad: float32 [4096, 1024], P(('replica', 'shard'))
- down_bias_grad: float32 [1024], P(('replica', 'shard'))
- mlp_scale_grad: float32 [1024], P(('replica', 'shard'))
The draws below stay inside these ranges and needn't reach their ends.
All inputs are finite; a program needn't handle non-finite values.
Results may differ from the reference program's by a relative error of at most 0.01.
Values may be sent and summed in bfloat16 or wider, within the bound.
No kernel may reach another device: no remote copies, remote signals or barrier semaphores. Data moves between devices by JAX's collectives and lax.ppermute only.
A program may use at most 192 MiB of HBM per device.

```python
import math
import jax
import jax.numpy as jnp
from jax import lax

D = 1024
HEADS = 16
HEAD_DIM = 64
FF = 4096
LENGTH = 325
IMAGES = 32
TOKENS = 10400


def with_spikes(array, own_key, source, target, parts, factor):
    def block_of(axis_at):
        return (jnp.arange(array.shape[axis_at]) // (array.shape[axis_at] // parts)).reshape((-1,) + (1,) * (array.ndim - 1 - axis_at))

    first = jax.random.permutation(own_key, parts)[block_of(target)]
    second = (block_of(target) + parts // 2) % parts
    return jnp.where((block_of(source) == first) | (block_of(source) == second), factor * array, array)


def shard_levels(rng, extent, split, least, high):
    factor_of = 1.0
    for position, blocks in split:
        heights = jax.random.uniform(jax.random.fold_in(jax.random.fold_in(rng, 6), position), (blocks,), jnp.float32, least / len(split), high / len(split))
        factor_of = factor_of * jnp.repeat(jnp.exp(heights), extent[position] // blocks).reshape((-1,) + (1,) * (len(extent) - 1 - position))
    return factor_of


def bell_draw(rng, extent, width, limit, split=(), kind=jnp.bfloat16):
    level = shard_levels(rng, extent, split, -0.22, 0.18) if split else 1.0
    values = jax.random.normal(rng, extent, jnp.float32) * width * level
    return jnp.minimum(jnp.maximum(values, -limit), limit).astype(kind)


def bell_draw_with(key, extent, scale, reach, pieces, heavy, dtype=jnp.bfloat16):
    drawn = scale * jax.random.normal(key, extent, jnp.float32)
    if pieces:
        drawn = drawn * shard_levels(key, extent, pieces, -0.22, 0.18)
    return jnp.clip(with_spikes(drawn, jax.random.fold_in(key, 3), *heavy), -reach, reach).astype(dtype)


def setup_inputs(seed: int = 0) -> dict:
    splits = jax.random.split(jax.random.key(seed), 18)
    return {
        "block_input": bell_draw_with(splits[0], (TOKENS, D), 1.0, 6.0, ((0, 32),), (0, 1, 32, 2.75), jnp.float32),
        "norm1_gain": jnp.clip(1.0 + 0.1 * jax.random.normal(splits[1], (D,), jnp.float32), 0.5, 1.5).astype(jnp.bfloat16),
        "norm1_bias": bell_draw(splits[2], (D,), 0.5, 3.0, ((0, 2),)),
        "qkv_weight": bell_draw(splits[3], (D, 3 * D), D ** -0.5, 0.1875, ((0, 2),)),
        "query_bias": bell_draw(splits[4], (D,), 0.5, 3.0, ((0, 2),)),
        "value_bias": bell_draw(splits[5], (D,), 0.5, 3.0, ((0, 2),)),
        "proj_weight": bell_draw(splits[6], (D, D), (D // 16) ** -0.5, 0.75, ((0, 2),)),
        "proj_bias": bell_draw(splits[7], (D,), 0.5, 3.0, ((0, 2),)),
        "attn_scale": jnp.clip(jnp.exp(math.log(1.5) - 1.6133518 * jax.random.uniform(splits[8], (D,), jnp.float32) ** shard_levels(splits[8], (D,), ((0, 2),), -0.2, 0.2)), 0.29882812, 1.5).astype(jnp.bfloat16),
        "norm2_gain": jnp.clip(1.0 + 0.1 * jax.random.normal(splits[9], (D,), jnp.float32), 0.5, 1.5).astype(jnp.bfloat16),
        "norm2_bias": bell_draw(splits[10], (D,), 0.5, 3.0, ((0, 2),)),
        "up_weight": bell_draw(splits[11], (D, FF), D ** -0.5, 0.1875, ((0, 2),)),
        "up_bias": bell_draw(splits[12], (FF,), 0.5, 3.0, ((0, 2),)),
        "down_weight": bell_draw(splits[13], (FF, D), FF ** -0.5, 0.09375, ((0, 2),)),
        "down_bias": bell_draw(splits[14], (D,), 0.5, 3.0, ((0, 2),)),
        "mlp_scale": jnp.clip(jnp.exp(math.log(1.5) - 1.6133518 * jax.random.uniform(splits[15], (D,), jnp.float32) ** shard_levels(splits[15], (D,), ((0, 2),), -0.2, 0.2)), 0.29882812, 1.5).astype(jnp.bfloat16),
        "out_grad": bell_draw(splits[16], (TOKENS, D), 1.0, 6.0, ((0, 32),), jnp.float32),
    }


norm_eps = 1e-06
root_half = 0.7071067811865476
inverse_root_two_pi = 0.3989422804014327

def product(form, left, right):
    return jnp.einsum(form, left.astype(jnp.float32), right.astype(jnp.float32))

def layer_norm(values, gain, shift):
    center = values - lax.optimization_barrier(jnp.mean(values, axis=-1, keepdims=True))
    spread = lax.rsqrt(lax.optimization_barrier(jnp.mean(center * center, axis=-1, keepdims=True)) + norm_eps)
    normed = center * spread
    return (normed, spread, normed * gain + shift)

def norm_back(grad_out, normed, spread, gain):
    scaled = grad_out * gain
    return spread * (scaled - lax.optimization_barrier(jnp.mean(scaled, axis=-1, keepdims=True)) - normed * lax.optimization_barrier(jnp.mean(scaled * normed, axis=-1, keepdims=True)))

def gelu_slope(values):
    return 0.5 * (1.0 + lax.erf(values * root_half)) + values * jnp.exp(-0.5 * values * values) * inverse_root_two_pi

def prepare(raw_params):
    return tuple((item if item.ndim == 2 else item.astype(jnp.float32) for item in raw_params))

def forward(inputs, params):
    gain_one, shift_one, qkv_mat, query_bias, value_bias, proj_mat, proj_bias, scale_one, gain_two, shift_two, up_mat, up_bias, down_mat, down_bias, scale_two = params
    lead_shape = inputs.shape[:2]
    factor = 1.0 / math.sqrt(HEAD_DIM)
    normed_one, spread_one, lifted = layer_norm(inputs, gain_one, shift_one)
    first = lifted.astype(jnp.bfloat16)
    mixed = product('bld,de->ble', first, qkv_mat)
    queries = ((mixed[..., :D] + query_bias) * factor).astype(jnp.bfloat16).reshape(lead_shape + (HEADS, HEAD_DIM))
    key_rows = mixed[..., D:2 * D].astype(jnp.bfloat16).reshape(lead_shape + (HEADS, HEAD_DIM))
    value_rows = (mixed[..., 2 * D:] + value_bias).astype(jnp.bfloat16).reshape(lead_shape + (HEADS, HEAD_DIM))
    scores = product('bqhe,bkhe->bhqk', queries, key_rows)
    logsum = jnp.log(lax.optimization_barrier(jnp.sum(jnp.exp(scores), axis=-1, keepdims=True)))
    attn_probs = jnp.exp(scores - logsum).astype(jnp.bfloat16)
    attended = product('bhqk,bkhe->bqhe', attn_probs, value_rows).reshape(lead_shape + (D,)).astype(jnp.bfloat16)
    branch = product('bld,de->ble', attended, proj_mat) + proj_bias
    middle = inputs + scale_one * branch
    normed_two, spread_two, lifted_two = layer_norm(middle, gain_two, shift_two)
    second = lifted_two.astype(jnp.bfloat16)
    before = product('bld,df->blf', second, up_mat) + up_bias
    hidden = (0.5 * before * (1.0 + lax.erf(before * root_half))).astype(jnp.bfloat16)
    result = product('blf,fd->bld', hidden, down_mat) + down_bias
    output = middle + scale_two * result
    saved = (normed_one, spread_one, first, queries, key_rows, value_rows, logsum, attended, branch, normed_two, spread_two, second, before, hidden, result)
    return (output, saved)

def backward(cotangent, params, saved):
    gain_one, shift_one, qkv_mat, query_bias, value_bias, proj_mat, proj_bias, scale_one, gain_two, shift_two, up_mat, up_bias, down_mat, down_bias, scale_two = params
    normed_one, spread_one, first, queries, key_rows, value_rows, logsum, attended, branch, normed_two, spread_two, second, before, hidden, result = saved
    lead_shape = cotangent.shape[:2]
    factor = 1.0 / math.sqrt(HEAD_DIM)
    grad_scale_two = lax.optimization_barrier(jnp.sum(cotangent * result, axis=(0, 1)))
    grad_result = cotangent * scale_two
    grad_down_bias = lax.optimization_barrier(jnp.sum(grad_result, axis=(0, 1)))
    grad_result_low = grad_result.astype(jnp.bfloat16)
    grad_down = product('blf,bld->fd', hidden, grad_result_low)
    grad_hidden = product('bld,fd->blf', grad_result_low, down_mat)
    grad_before = grad_hidden * gelu_slope(before)
    grad_up_bias = lax.optimization_barrier(jnp.sum(grad_before, axis=(0, 1)))
    grad_before_low = grad_before.astype(jnp.bfloat16)
    grad_up = product('bld,blf->df', second, grad_before_low)
    grad_lifted_two = product('blf,df->bld', grad_before_low, up_mat)
    grad_gain_two = lax.optimization_barrier(jnp.sum(grad_lifted_two * normed_two, axis=(0, 1)))
    grad_shift_two = lax.optimization_barrier(jnp.sum(grad_lifted_two, axis=(0, 1)))
    grad_middle = cotangent + norm_back(grad_lifted_two, normed_two, spread_two, gain_two)
    grad_scale_one = lax.optimization_barrier(jnp.sum(grad_middle * branch, axis=(0, 1)))
    grad_branch = grad_middle * scale_one
    grad_proj_bias = lax.optimization_barrier(jnp.sum(grad_branch, axis=(0, 1)))
    grad_branch_low = grad_branch.astype(jnp.bfloat16)
    grad_proj = product('bld,ble->de', attended, grad_branch_low)
    grad_attended = product('ble,de->bld', grad_branch_low, proj_mat).astype(jnp.bfloat16).reshape(lead_shape + (HEADS, HEAD_DIM))
    scores = product('bqhe,bkhe->bhqk', queries, key_rows)
    exact_probs = jnp.exp(scores - logsum)
    attn_probs = exact_probs.astype(jnp.bfloat16)
    grad_values = product('bhqk,bqhe->bkhe', attn_probs, grad_attended).reshape(lead_shape + (D,))
    grad_probs = product('bqhe,bkhe->bhqk', grad_attended, value_rows)
    grad_scores = (exact_probs * (grad_probs - lax.optimization_barrier(jnp.sum(exact_probs * grad_probs, axis=-1, keepdims=True)))).astype(jnp.bfloat16)
    grad_queries = (product('bhqk,bkhe->bqhe', grad_scores, key_rows) * factor).reshape(lead_shape + (D,))
    grad_keys = product('bhqk,bqhe->bkhe', grad_scores, queries).reshape(lead_shape + (D,))
    grad_query_bias = lax.optimization_barrier(jnp.sum(grad_queries, axis=(0, 1)))
    grad_value_bias = lax.optimization_barrier(jnp.sum(grad_values, axis=(0, 1)))
    grad_mixed_low = jnp.concatenate([grad_queries, grad_keys, grad_values], axis=-1).astype(jnp.bfloat16)
    grad_qkv = product('bld,ble->de', first, grad_mixed_low)
    grad_lifted_one = product('ble,de->bld', grad_mixed_low, qkv_mat)
    grad_gain_one = lax.optimization_barrier(jnp.sum(grad_lifted_one * normed_one, axis=(0, 1)))
    grad_shift_one = lax.optimization_barrier(jnp.sum(grad_lifted_one, axis=(0, 1)))
    grad_input = grad_middle + norm_back(grad_lifted_one, normed_one, spread_one, gain_one)
    gradients = (grad_gain_one, grad_shift_one, grad_qkv, grad_query_bias, grad_value_bias, grad_proj, grad_proj_bias, grad_scale_one, grad_gain_two, grad_shift_two, grad_up, grad_up_bias, grad_down, grad_down_bias, grad_scale_two)
    return (grad_input, gradients)

def reference(block_input, norm1_gain, norm1_bias, qkv_weight, query_bias, value_bias, proj_weight, proj_bias, attn_scale, norm2_gain, norm2_bias, up_weight, up_bias, down_weight, down_bias, mlp_scale, out_grad):
    params = prepare((norm1_gain, norm1_bias, qkv_weight, query_bias, value_bias, proj_weight, proj_bias, attn_scale, norm2_gain, norm2_bias, up_weight, up_bias, down_weight, down_bias, mlp_scale))
    inputs = block_input.reshape(IMAGES, 1, LENGTH, D)
    cotangents = out_grad.reshape(IMAGES, 1, LENGTH, D)

    def image_step(totals, carried):
        output, saved = forward(carried[0], params)
        grad_input, gradients = backward(carried[1], params, saved)
        return (tuple((a + b for a, b in zip(totals, gradients))), (output, grad_input))
    initial = tuple((jnp.zeros(item.shape, jnp.float32) for item in params))
    totals, outcome = lax.scan(image_step, initial, (inputs, cotangents))
    outputs = outcome[0].reshape(TOKENS, D)
    grad_inputs = outcome[1].reshape(TOKENS, D)
    return (outputs, grad_inputs, totals[0], totals[1], totals[2], totals[3], totals[4], totals[5], totals[6], totals[7], totals[8], totals[9], totals[10], totals[11], totals[12], totals[13], totals[14])
```

```python
import math

import jax
import jax.numpy as jnp
from jax import lax
from jax.sharding import PartitionSpec as P

D = 1024
HEADS = 16
HEAD_DIM = 64
LENGTH = 325


norm_eps = 1e-06
root_half = 0.7071067811865476
inverse_root_two_pi = 0.3989422804014327


def partner_2(value, axis, bit):
    mask = 2**bit
    pairs = [(source, source ^ mask) for source in range(lax.axis_size(axis))]
    return lax.ppermute(value, axis, pairs)


def product(form, left, right):
    return jnp.einsum(form, left, right, preferred_element_type=jnp.float32)


def layer_norm(values, gain, shift):
    center = values - jnp.mean(values, axis=-1, keepdims=True)
    spread = lax.rsqrt(jnp.mean(center * center, axis=-1, keepdims=True) + norm_eps)
    normed = center * spread
    return (normed, spread, normed * gain + shift)


def norm_back(grad_out, normed, spread, gain):
    scaled = grad_out * gain
    return spread * (
        scaled
        - jnp.mean(scaled, axis=-1, keepdims=True)
        - normed * jnp.mean(scaled * normed, axis=-1, keepdims=True)
    )


def gelu_slope(values):
    return (
        0.5 * (1.0 + lax.erf(values * root_half))
        + values * jnp.exp(-0.5 * values * values) * inverse_root_two_pi
    )


def prepare(raw_params):
    return tuple((item if item.ndim == 2 else item.astype(jnp.float32) for item in raw_params))


def forward(inputs, params):
    (
        gain_one,
        shift_one,
        qkv_mat,
        query_bias,
        value_bias,
        proj_mat,
        proj_bias,
        scale_one,
        gain_two,
        shift_two,
        up_mat,
        up_bias,
        down_mat,
        down_bias,
        scale_two,
    ) = params
    lead_shape = inputs.shape[:2]
    factor = 1.0 / math.sqrt(HEAD_DIM)
    normed_one, spread_one, lifted = layer_norm(inputs, gain_one, shift_one)
    first = lifted.astype(jnp.bfloat16)
    mixed = product("bld,de->ble", first, qkv_mat)
    queries = (
        ((mixed[..., :D] + query_bias) * factor)
        .astype(jnp.bfloat16)
        .reshape(lead_shape + (HEADS, HEAD_DIM))
    )
    key_rows = mixed[..., D : 2 * D].astype(jnp.bfloat16).reshape(lead_shape + (HEADS, HEAD_DIM))
    value_rows = (
        (mixed[..., 2 * D :] + value_bias)
        .astype(jnp.bfloat16)
        .reshape(lead_shape + (HEADS, HEAD_DIM))
    )
    scores = product("bqhe,bkhe->bhqk", queries, key_rows)
    logsum = jnp.log(jnp.sum(jnp.exp(scores), axis=-1, keepdims=True))
    attn_probs = jnp.exp(scores - logsum).astype(jnp.bfloat16)
    attended = (
        product("bhqk,bkhe->bqhe", attn_probs, value_rows)
        .reshape(lead_shape + (D,))
        .astype(jnp.bfloat16)
    )
    branch = product("bld,de->ble", attended, proj_mat) + proj_bias
    middle = inputs + scale_one * branch
    normed_two, spread_two, lifted_two = layer_norm(middle, gain_two, shift_two)
    second = lifted_two.astype(jnp.bfloat16)
    before = product("bld,df->blf", second, up_mat) + up_bias
    hidden = (0.5 * before * (1.0 + lax.erf(before * root_half))).astype(jnp.bfloat16)
    result = product("blf,fd->bld", hidden, down_mat) + down_bias
    output = middle + scale_two * result
    saved = (
        normed_one,
        spread_one,
        first,
        queries,
        key_rows,
        value_rows,
        logsum,
        attended,
        branch,
        normed_two,
        spread_two,
        second,
        before,
        hidden,
        result,
    )
    return (output, saved)


def backward(cotangent, params, saved):
    (
        gain_one,
        shift_one,
        qkv_mat,
        query_bias,
        value_bias,
        proj_mat,
        proj_bias,
        scale_one,
        gain_two,
        shift_two,
        up_mat,
        up_bias,
        down_mat,
        down_bias,
        scale_two,
    ) = params
    (
        normed_one,
        spread_one,
        first,
        queries,
        key_rows,
        value_rows,
        logsum,
        attended,
        branch,
        normed_two,
        spread_two,
        second,
        before,
        hidden,
        result,
    ) = saved
    lead_shape = cotangent.shape[:2]
    factor = 1.0 / math.sqrt(HEAD_DIM)
    grad_scale_two = jnp.sum(cotangent * result, axis=(0, 1))
    grad_result = cotangent * scale_two
    grad_down_bias = jnp.sum(grad_result, axis=(0, 1))
    grad_result_low = grad_result.astype(jnp.bfloat16)
    grad_down = product("blf,bld->fd", hidden, grad_result_low)
    grad_hidden = product("bld,fd->blf", grad_result_low, down_mat)
    grad_before = grad_hidden * gelu_slope(before)
    grad_up_bias = jnp.sum(grad_before, axis=(0, 1))
    grad_before_low = grad_before.astype(jnp.bfloat16)
    grad_up = product("bld,blf->df", second, grad_before_low)
    grad_lifted_two = product("blf,df->bld", grad_before_low, up_mat)
    grad_gain_two = jnp.sum(grad_lifted_two * normed_two, axis=(0, 1))
    grad_shift_two = jnp.sum(grad_lifted_two, axis=(0, 1))
    grad_middle = cotangent + norm_back(grad_lifted_two, normed_two, spread_two, gain_two)
    grad_scale_one = jnp.sum(grad_middle * branch, axis=(0, 1))
    grad_branch = grad_middle * scale_one
    grad_proj_bias = jnp.sum(grad_branch, axis=(0, 1))
    grad_branch_low = grad_branch.astype(jnp.bfloat16)
    grad_proj = product("bld,ble->de", attended, grad_branch_low)
    grad_attended = (
        product("ble,de->bld", grad_branch_low, proj_mat)
        .astype(jnp.bfloat16)
        .reshape(lead_shape + (HEADS, HEAD_DIM))
    )
    scores = product("bqhe,bkhe->bhqk", queries, key_rows)
    exact_probs = jnp.exp(scores - logsum)
    attn_probs = exact_probs.astype(jnp.bfloat16)
    grad_values = product("bhqk,bqhe->bkhe", attn_probs, grad_attended).reshape(lead_shape + (D,))
    grad_probs = product("bqhe,bkhe->bhqk", grad_attended, value_rows)
    grad_scores = (
        exact_probs * (grad_probs - jnp.sum(exact_probs * grad_probs, axis=-1, keepdims=True))
    ).astype(jnp.bfloat16)
    grad_queries = (product("bhqk,bkhe->bqhe", grad_scores, key_rows) * factor).reshape(
        lead_shape + (D,)
    )
    grad_keys = product("bhqk,bqhe->bkhe", grad_scores, queries).reshape(lead_shape + (D,))
    grad_query_bias = jnp.sum(grad_queries, axis=(0, 1))
    grad_value_bias = jnp.sum(grad_values, axis=(0, 1))
    grad_mixed_low = jnp.concatenate([grad_queries, grad_keys, grad_values], axis=-1).astype(
        jnp.bfloat16
    )
    grad_qkv = product("bld,ble->de", first, grad_mixed_low)
    grad_lifted_one = product("ble,de->bld", grad_mixed_low, qkv_mat)
    grad_gain_one = jnp.sum(grad_lifted_one * normed_one, axis=(0, 1))
    grad_shift_one = jnp.sum(grad_lifted_one, axis=(0, 1))
    grad_input = grad_middle + norm_back(grad_lifted_one, normed_one, spread_one, gain_one)
    gradients = (
        grad_gain_one,
        grad_shift_one,
        grad_qkv,
        grad_query_bias,
        grad_value_bias,
        grad_proj,
        grad_proj_bias,
        grad_scale_one,
        grad_gain_two,
        grad_shift_two,
        grad_up,
        grad_up_bias,
        grad_down,
        grad_down_bias,
        grad_scale_two,
    )
    lowered = (grad_mixed_low, grad_branch_low, grad_before_low, grad_result_low)
    return (grad_input, gradients, lowered)


VECTOR_SLOTS = (0, 1, 3, 4, 6, 7, 8, 9, 11, 13, 14)
MATRIX_SLOTS = (2, 5, 10, 12)


def bit_orders(replicas):
    count = replicas.bit_length() - 1
    bits = list(range(count))
    if count < 3:
        return (bits, bits, bits)
    rest = bits[3:]
    return ([0, 1, 2] + rest, [1, 2, 0] + rest, [2, 0, 1] + rest)


def halve(values, order, axis):
    size = lax.axis_size(axis)
    count = size.bit_length() - 1
    tail = values.shape[1:]
    current = values.reshape((2,) * count + tail)
    left = list(range(count - 1, -1, -1))
    for bit in order:
        place = left.index(bit)
        away = lax.index_in_dim(current, 1, place, keepdims=False)
        keep = lax.index_in_dim(current, 0, place, keepdims=False)
        current = keep + partner_2(away, axis, bit)
        left.remove(bit)
    return current


def column_parts(width):
    tiles = width // 128
    first = max(1, round(tiles * 0.43))
    second = max(1, round(tiles * 0.36))
    return (first * 128, second * 128, width - (first + second) * 128)


def on_device(*args):
    block_input, raw, out_grad = args[0], args[1:16], args[16]
    replicas = lax.axis_size("replica")
    mine = lax.axis_index("shard")
    me = lax.axis_index("replica")
    first_half = mine == 0

    def join(own, other):
        return jnp.concatenate(
            [jnp.where(first_half, own, other), jnp.where(first_half, other, own)], axis=0
        )

    vectors = [raw[slot] for slot in VECTOR_SLOTS]
    packed = jnp.concatenate(vectors)
    packed_other = partner_2(packed, "shard", 0)
    full = [None] * 15
    at = 0
    for slot, own in zip(VECTOR_SLOTS, vectors):
        full[slot] = join(own, packed_other[at : at + own.shape[0]])
        at += own.shape[0]
    for slot in MATRIX_SLOTS:
        full[slot] = join(raw[slot], partner_2(raw[slot], "shard", 0))
    params = prepare(full)
    inputs = block_input.reshape(-1, LENGTH, D)
    output, saved = forward(inputs, params)
    grad_input, gradients, lowered = backward(out_grad.reshape(-1, LENGTH, D), params, saved)
    lefts = (saved[2], saved[7], saved[11], saved[13])

    def pick(values, owner):
        width = values.shape[-1]
        block = width // (2 * replicas)
        target = lax.broadcasted_iota(jnp.int32, (width, width // 2), 1)
        source = lax.broadcasted_iota(jnp.int32, (width, width // 2), 0)
        wanted = ((target // block) ^ me) * (2 * block) + owner * block + target % block
        chooser = (source == wanted).astype(jnp.bfloat16)
        return product("bld,de->ble", values, chooser).astype(jnp.bfloat16)

    def pick_wide(values, owner):
        width = values.shape[-1]
        block = width // (2 * replicas)
        split = values.reshape(values.shape[:-1] + (replicas, 2, block))
        taken = lax.dynamic_index_in_dim(split, owner, axis=3, keepdims=False)
        order = jnp.arange(replicas) ^ me
        return jnp.take(taken, order, axis=2).reshape(values.shape[:-1] + (width // 2,))

    halves = {}
    for slot, left, right in zip(MATRIX_SLOTS, lefts, lowered):
        chosen = pick_wide if slot == 12 and left.shape[-1] // (2 * replicas) % 128 == 0 else pick
        own_left = chosen(left, mine)
        their_left = partner_2(chosen(left, 1 - mine), "shard", 0)
        their_right = partner_2(right, "shard", 0)
        whole = product(
            "bld,ble->de",
            jnp.concatenate([own_left, their_left], axis=1),
            jnp.concatenate([right, their_right], axis=1),
        ).astype(jnp.bfloat16)
        halves[slot] = whole.reshape((replicas, -1) + whole.shape[1:])
    outs = [None] * 15
    orders = bit_orders(replicas)
    for slot in (12, 10, 5, 2):
        pieces = []
        at = 0
        for width, order in zip(column_parts(halves[slot].shape[-1]), orders):
            pieces.append(halve(halves[slot][..., at : at + width], order, "replica"))
            at += width
        outs[slot] = jnp.concatenate(pieces, axis=-1).astype(jnp.float32)
    rows = []
    for slot in VECTOR_SLOTS:
        total = gradients[slot]
        rows.append(total.reshape(replicas, 2, -1))
    stacked = jnp.concatenate(rows, axis=2)
    theirs = lax.dynamic_index_in_dim(stacked, 1 - mine, 1, keepdims=False)
    ours = lax.dynamic_index_in_dim(stacked, mine, 1, keepdims=False)
    joined = ours + partner_2(theirs, "shard", 0)
    relative = jnp.take(joined, jnp.arange(replicas) ^ me, axis=0)
    summed = halve(relative, orders[0], "replica")
    at = 0
    for slot, part in zip(VECTOR_SLOTS, rows):
        outs[slot] = summed[at : at + part.shape[2]]
        at += part.shape[2]
    return (output.reshape(-1, D), grad_input.reshape(-1, D)) + tuple(outs)


def solution(mesh):
    placed = (
        P(("replica", "shard"), None),
        P("shard"),
        P("shard"),
        P("shard", None),
        P("shard"),
        P("shard"),
        P("shard", None),
        P("shard"),
        P("shard"),
        P("shard"),
        P("shard"),
        P("shard", None),
        P("shard"),
        P("shard", None),
        P("shard"),
        P("shard"),
        P(("replica", "shard"), None),
    )
    return jax.shard_map(
        on_device,
        mesh=mesh,
        in_specs=placed,
        out_specs=(
            P(("replica", "shard"), None),
            P(("replica", "shard"), None),
            P(("replica", "shard")),
            P(("replica", "shard")),
            P(("replica", "shard"), None),
            P(("replica", "shard")),
            P(("replica", "shard")),
            P(("replica", "shard"), None),
            P(("replica", "shard")),
            P(("replica", "shard")),
            P(("replica", "shard")),
            P(("replica", "shard")),
            P(("replica", "shard"), None),
            P(("replica", "shard")),
            P(("replica", "shard"), None),
            P(("replica", "shard")),
            P(("replica", "shard")),
        ),
        check_vma=False,
    )
```
